32 devices in a mesh: groups: 2 (over y), tok: 4 (over z), slot: 2 (over x), hid: 2 (over core).
Axes of the slice: x: 2, y: 2, z: 4, core: 2. Of those that a mesh axis runs over, the one named last changes fastest.
Arguments:
- tokens: bfloat16 [8192, 1024], P(('groups', 'tok', 'slot', 'hid')), parts along dimension 0, may hold values from -12 to 12
- slot_keys: bfloat16 [2048, 512], P('groups', 'slot'), parts along dimension 0, may hold values from -12 to 12
- w_in: bfloat16 [4, 4, 1024, 4096], P(('groups', 'slot'), 'tok', None, 'hid'), parts along dimension 0, may hold values from -0.1875 to 0.1875
- w_out: bfloat16 [4, 4, 4096, 1024], P(('groups', 'slot'), 'tok', 'hid'), parts along dimension 0, may hold values from -0.09375 to 0.09375
Outputs:
- mixed: float32 [8192, 1024], P(('groups', 'tok', 'slot', 'hid')), parts along dimension 0
The draws below stay inside these ranges and needn't reach their ends.
There are 2 independent parts, one for each index of `groups`. The reference program is written for one: setup_inputs(seed, part) draws one part's arguments, and reference() takes and returns one part's arrays. A program takes and returns all parts, laid end to end along the dimension named above; each array names one. Nothing has to cross between parts.
All inputs are finite; a program needn't handle non-finite values.
Results may differ from the reference program's by a relative error of at most 0.0022.
Values may be sent and summed in bfloat16 or wider, within the bound.
No kernel may reach another device: no remote copies, remote signals or barrier semaphores. Data moves between devices by JAX's collectives and lax.ppermute only.
A program may use at most 64 MiB of HBM per device.

```python
import jax
import jax.numpy as jnp
from jax import lax

D = 1024
H = 4096
SLOTS = 64
BLOCKS = 2
PER_BLOCK = 4
S = 512
TOKENS = 4096


def cluster_centres(key):
    return jax.random.normal(jax.random.fold_in(key, 11), (64, D), jnp.float32)


def draw_tokens(key, part):
    centres = cluster_centres(key)
    member = jax.random.randint(jax.random.fold_in(key, 12), (TOKENS,), 0, 64)
    noise = jax.random.normal(jax.random.fold_in(key, 13), (TOKENS, D), jnp.float32)
    base = 1.5 * jnp.take(centres, member, axis=0) + noise
    row_scale = jax.random.uniform(jax.random.fold_in(key, 14), (TOKENS, 1), jnp.float32, 0.6, 1.6)
    base = row_scale * base
    return jnp.clip(base, -12.0, 12.0).astype(jnp.bfloat16)


def draw_slot_keys(key, part):
    centres = cluster_centres(key)
    member = jax.random.randint(jax.random.fold_in(key, 16), (S,), 0, 64)
    noise = jax.random.normal(jax.random.fold_in(key, 17), (D, S), jnp.float32)
    base = 1.5 * jnp.take(centres, member, axis=0).T + noise
    return jnp.clip(base, -12.0, 12.0).astype(jnp.bfloat16)


def level_of(key, dims, split, low, top_value):
    factor_of = 1.0
    for dim, parts in split:
        draws = jax.random.uniform(jax.random.fold_in(jax.random.fold_in(key, 6), dim), (parts,), jnp.float32, low / len(split), top_value / len(split))
        factor_of = factor_of * jnp.repeat(jnp.exp(draws), dims[dim] // parts).reshape((-1,) + (1,) * (len(dims) - 1 - dim))
    return factor_of


def normal_values(stream_key, extent, deviation, most, split=(), dtype=jnp.bfloat16):
    entries = deviation * jax.random.normal(stream_key, extent, jnp.float32)
    if split:
        entries = entries * level_of(stream_key, extent, split, -0.22, 0.18)
    return jnp.clip(entries, -most, most).astype(dtype)


def setup_inputs(seed: int = 0, part: int = 0) -> dict:
    keys = jax.random.split(jax.random.key(seed), 5)
    part_keys = jax.random.split(jax.random.fold_in(keys[4], part), 5)
    return {
        "tokens": draw_tokens(jax.random.fold_in(jax.random.fold_in(keys[4], part), 71), part),
        "slot_keys": draw_slot_keys(jax.random.fold_in(jax.random.fold_in(keys[4], part), 71), part),
        "w_in": normal_values(part_keys[2], (BLOCKS, PER_BLOCK, D, H), D ** -0.5, 0.1875, ((0, 2), (1, 4), (3, 2))),
        "w_out": normal_values(part_keys[3], (BLOCKS, PER_BLOCK, H, D), H ** -0.5, 0.09375, ((0, 2), (1, 4), (2, 2))),
    }


epsilon = 1e-06

def block_weights(tokens, token_scale, key_block, scale_block):
    logits = 4.0 * token_scale[:, None] * scale_block[None, :] * jnp.dot(tokens, key_block, preferred_element_type=jnp.float32) / D
    return jnp.exp(logits)

def reference(tokens, slot_keys, w_in, w_out):
    token_scale = lax.rsqrt(lax.optimization_barrier(jnp.mean(jnp.square(tokens.astype(jnp.float32)), axis=1)) + epsilon)
    key_scale = lax.rsqrt(lax.optimization_barrier(jnp.mean(jnp.square(slot_keys.astype(jnp.float32)), axis=0)) + epsilon)
    width = S // BLOCKS
    key_blocks = slot_keys.reshape(D, BLOCKS, width).transpose(1, 0, 2)
    scale_blocks = key_scale.reshape(BLOCKS, width)

    def first_pass(carry, items):
        key_block, scale_block = items
        weights_exp = block_weights(tokens, token_scale, key_block, scale_block)
        weights_low = weights_exp.astype(jnp.bfloat16)
        numer = lax.dot_general(weights_low, tokens, (((0,), (0,)), ((), ())), preferred_element_type=jnp.float32)
        inputs = (numer / lax.optimization_barrier(jnp.sum(weights_exp, axis=0))[:, None]).astype(jnp.bfloat16)
        return (carry + lax.optimization_barrier(jnp.sum(weights_exp, axis=1)), inputs)
    token_totals, slot_inputs = lax.scan(first_pass, jnp.zeros((TOKENS,), jnp.float32), (key_blocks, scale_blocks))
    slot_inputs = slot_inputs.reshape(BLOCKS, PER_BLOCK, SLOTS, D)

    def run_block(items):
        inputs, first_w, second_w = items
        hidden = jax.nn.gelu(jnp.einsum('asd,adh->ash', inputs.astype(jnp.float32), first_w.astype(jnp.float32)), approximate=True).astype(jnp.bfloat16)
        return jnp.einsum('ash,ahd->asd', hidden.astype(jnp.float32), second_w.astype(jnp.float32)).astype(jnp.bfloat16)
    slot_outputs = lax.map(run_block, (slot_inputs, w_in, w_out)).reshape(BLOCKS, width, D)

    def second_pass(carry, items):
        key_block, scale_block, outputs = items
        weights_low = block_weights(tokens, token_scale, key_block, scale_block).astype(jnp.bfloat16)
        return (carry + jnp.dot(weights_low, outputs, preferred_element_type=jnp.float32), 0)
    numer, unused = lax.scan(second_pass, jnp.zeros((TOKENS, D), jnp.float32), (key_blocks, scale_blocks, slot_outputs))
    return numer / token_totals[:, None]
```

```python
import functools

import jax
import jax.numpy as jnp
from jax import lax
from jax.experimental import pallas as pl
from jax.experimental.pallas import tpu as pltpu
from jax.sharding import PartitionSpec as P

epsilon = 1e-06
bf16, f32 = jnp.bfloat16, jnp.float32
VMEM = pl.BlockSpec(memory_space=pltpu.VMEM)


def call(body, outs, *args, name, flops=0, nbytes=0):
    return pl.pallas_call(
        body,
        out_shape=[jax.ShapeDtypeStruct(s, d) for s, d in outs],
        in_specs=[VMEM] * len(args),
        out_specs=[VMEM] * len(outs),
        name=name,
        compiler_params=pltpu.CompilerParams(vmem_limit_bytes=40 * 2**20),
        cost_estimate=pl.CostEstimate(flops=flops, bytes_accessed=nbytes, transcendentals=0),
    )(*args)


def shift(value, axis, step):
    count = lax.axis_size(axis)
    return lax.ppermute(value, axis, [(i, (i + step) % count) for i in range(count)])


def dispatch_body(first, half, *refs):
    if first:
        tok_ref, key_ref, low_ref, keep_ref, send_ref = refs
    else:
        tok_ref, key_ref, keep_in, send_in, low_ref, keep_ref, send_ref = refs
    width = tok_ref.shape[1]
    slots = key_ref.shape[1]
    core = lax.axis_index("hid")
    tok = tok_ref[...].astype(f32)
    key = key_ref[...].astype(f32)
    tok_scale = lax.rsqrt(jnp.sum(tok * tok, axis=1, keepdims=True) / width + epsilon)
    key_scale = lax.rsqrt(jnp.sum(key * key, axis=0, keepdims=True) / width + epsilon)
    logits = jnp.dot(tok_ref[...], key_ref[...], preferred_element_type=f32)
    weights = jnp.exp(logits * (tok_scale * (4.0 / width)) * key_scale)
    low = weights.astype(bf16)
    low_ref[...] = low
    mine = pl.ds(pl.multiple_of(core * half, half), half)
    other = pl.ds(pl.multiple_of((1 - core) * half, half), half)
    dims = (((0,), (0,)), ((), ()))
    keep = lax.dot_general(low, tok_ref[:, mine], dims, preferred_element_type=f32)
    send = lax.dot_general(low, tok_ref[:, other], dims, preferred_element_type=f32)
    total = jnp.broadcast_to(jnp.sum(weights, axis=0, keepdims=True), (8, slots))
    if first:
        keep_ref[0:slots, :] = keep
        send_ref[0:slots, :] = send
        for ref in (keep_ref, send_ref):
            for at in range(0, slots, half):
                wide = min(half, slots - at)
                ref[slots + 8 * (at // half) : slots + 8 * (at // half) + 8, 0:wide] = total[:, at : at + wide]
    else:
        keep_ref[0:slots, :] = keep + keep_in[0:slots, :]
        send_ref[0:slots, :] = send + send_in[0:slots, :]
        for ref, old in ((keep_ref, keep_in), (send_ref, send_in)):
            for at in range(0, slots, half):
                wide = min(half, slots - at)
                rows = slice(slots + 8 * (at // half), slots + 8 * (at // half) + 8)
                ref[rows, 0:wide] = total[:, at : at + wide] + old[rows, 0:wide]


def share_body(owned, slots, keep_ref, recv_ref, mine_ref, total_ref, *send_refs):
    half = keep_ref.shape[1]
    row = lax.axis_index("tok")
    count = slots // owned
    for at in range(0, slots, half):
        wide = min(half, slots - at)
        rows = slice(slots + 8 * (at // half), slots + 8 * (at // half) + 8)
        total_ref[:, at : at + wide] = keep_ref[rows, 0:wide] + recv_ref[rows, 0:wide]
    for step in range(count):
        start = pl.multiple_of(lax.rem(row + step, count) * owned, owned)
        piece = keep_ref[pl.ds(start, owned), :] + recv_ref[pl.ds(start, owned), :]
        if step == 0:
            mine_ref[...] = piece
        else:
            send_refs[step - 1][...] = piece.astype(bf16)


def inputs_body(others, mine_ref, total_ref, *refs):
    piece_refs, total_refs, out_ref = refs[:others], refs[others : 2 * others], refs[2 * others]
    owned = mine_ref.shape[0]
    slots = total_ref.shape[1]
    numer = mine_ref[...]
    total = total_ref[0:1, :]
    for ref in piece_refs:
        numer = numer + ref[...].astype(f32)
    for ref in total_refs:
        total = total + ref[0:1, :]
    lane = lax.broadcasted_iota(jnp.int32, (owned, slots), 1)
    wanted = lax.broadcasted_iota(jnp.int32, (owned, slots), 0) + lax.axis_index("tok") * owned
    denom = jnp.sum(jnp.where(lane == wanted, jnp.broadcast_to(total, (owned, slots)), 0.0), axis=1, keepdims=True)
    out_ref[...] = (numer / denom).astype(bf16)


def expert_body(mine_ref, other_ref, in_ref, out_w_ref, out_ref):
    half = mine_ref.shape[1]
    core = lax.axis_index("hid")
    mine = pl.ds(pl.multiple_of(core * half, half), half)
    other = pl.ds(pl.multiple_of((1 - core) * half, half), half)
    value = jnp.dot(mine_ref[...], in_ref[mine, :], preferred_element_type=f32)
    value = value + jnp.dot(other_ref[...], in_ref[other, :], preferred_element_type=f32)
    hidden = jax.nn.gelu(value, approximate=True).astype(bf16)
    out_ref[...] = jnp.dot(hidden, out_w_ref[...], preferred_element_type=f32)


def outputs_body(part_ref, recv_ref, full_ref, half_ref):
    half = half_ref.shape[1]
    core = lax.axis_index("hid")
    full_ref[...] = (part_ref[...] + recv_ref[...]).astype(bf16)
    mine = pl.ds(pl.multiple_of(core * half, half), half)
    half_ref[...] = (part_ref[:, mine] + recv_ref[:, mine]).astype(bf16)


def combine_body(blocks, rows, *refs):
    low_refs = refs[:blocks]
    full_ref = refs[blocks]
    pieces = refs[blocks + 1 : -2]
    out_ref, all_ref = refs[-2], refs[-1]
    owned = full_ref.shape[0]
    half = full_ref.shape[1] // 2
    core = lax.axis_index("hid")
    row = lax.axis_index("tok")
    mine = pl.ds(pl.multiple_of(core * half, half), half)
    other = pl.ds(pl.multiple_of((1 - core) * half, half), half)
    at = 0
    for block in range(blocks):
        for step in range(rows):
            start = pl.ds(pl.multiple_of(lax.rem(row - step + rows, rows) * owned, owned), owned)
            if block == 0 and step == 0:
                all_ref[block, start, :] = full_ref[...]
                continue
            all_ref[block, start, mine] = pieces[at][...]
            all_ref[block, start, other] = pieces[at + 1][...]
            at += 2
    numer = None
    denom = None
    for block in range(blocks):
        low = low_refs[block][...]
        part = jnp.dot(low, all_ref[block], preferred_element_type=f32)
        total = jnp.sum(low.astype(f32), axis=1, keepdims=True)
        numer = part if numer is None else numer + part
        denom = total if denom is None else denom + total
    out_ref[...] = numer / denom


def local(tokens, slot_keys, w_in, w_out):
    count, width = tokens.shape
    slots = slot_keys.shape[1]
    rows, blocks = lax.axis_size("tok"), lax.axis_size("slot")
    owned = slots // rows
    half = width // 2
    extra = 8 * pl.cdiv(slots, half)
    part = ((slots + extra, half), f32)

    arrived = [shift(tokens, "slot", step) for step in range(1, blocks)]
    mac = 4 * count * width * slots
    low, keep, send = call(
        functools.partial(dispatch_body, True, half),
        [((count, slots), bf16), part, part],
        tokens, slot_keys, name="dispatch_own", flops=mac, nbytes=2 * count * width,
    )
    lows = [low]
    for step in range(1, blocks):
        low, keep, send = call(
            functools.partial(dispatch_body, False, half),
            [((count, slots), bf16), part, part],
            arrived[step - 1], slot_keys, keep, send, name="dispatch_other", flops=mac, nbytes=2 * count * width,
        )
        lows.append(shift(low, "slot", -step))
    recv = shift(send, "hid", 1)
    mine, total, *sends = call(
        functools.partial(share_body, owned, slots),
        [((owned, half), f32), ((8, slots), f32)] + [((owned, half), bf16)] * (rows - 1),
        keep, recv, name="share", nbytes=12 * slots * half,
    )
    totals = [shift(total, "tok", step) for step in range(1, rows)]
    pieces = [shift(sends[step - 1], "tok", step) for step in range(1, rows)]
    (inputs,) = call(
        functools.partial(inputs_body, rows - 1),
        [((owned, half), bf16)],
        mine, total, *pieces, *totals, name="slot_inputs", nbytes=8 * owned * width,
    )
    inputs_other = shift(inputs, "hid", 1)
    (outputs_part,) = call(
        expert_body, [((owned, width), f32)],
        inputs, inputs_other, w_in[0, 0], w_out[0, 0],
        name="expert", flops=4 * owned * width * w_in.shape[3], nbytes=4 * width * w_in.shape[3],
    )
    outputs_recv = shift(outputs_part, "hid", 1)
    full, mine_half = call(
        outputs_body, [((owned, width), bf16), ((owned, half), bf16)],
        outputs_part, outputs_recv, name="slot_outputs", nbytes=8 * owned * width,
    )
    chunks = [[mine_half] + [shift(mine_half, "tok", step) for step in range(1, rows)]]
    for step in range(1, blocks):
        chunks.append([shift(piece, "slot", step) for piece in chunks[0]])
    flat = [piece for block in range(blocks) for piece in chunks[block]][1:]
    pairs = []
    for piece in flat:
        pairs += [piece, shift(piece, "hid", 1)]
    order = [lows[0]] + [lows[(blocks - step) % blocks] for step in range(1, blocks)]
    return pl.pallas_call(
        functools.partial(combine_body, blocks, rows),
        out_shape=jax.ShapeDtypeStruct((count, width), f32),
        in_specs=[VMEM] * (blocks + 1 + len(pairs)),
        out_specs=VMEM,
        scratch_shapes=[pltpu.VMEM((blocks, slots, width), bf16)],
        name="combine",
        compiler_params=pltpu.CompilerParams(vmem_limit_bytes=40 * 2**20),
    )(*order, full, *pairs)


def solution(mesh):
    in_specs = (
        P(("groups", "tok", "slot", "hid"), None),
        P("groups", "slot"),
        P(("groups", "slot"), "tok", None, "hid"),
        P(("groups", "slot"), "tok", "hid", None),
    )
    out_specs = P(("groups", "tok", "slot", "hid"), None)
    return jax.shard_map(local, mesh=mesh, in_specs=in_specs, out_specs=out_specs, check_vma=False)
```

```python
import functools

import jax
import jax.numpy as jnp
from jax import lax
from jax.experimental import pallas as pl
from jax.experimental.pallas import tpu as pltpu
from jax.sharding import PartitionSpec as P

epsilon = 1e-06
bf16, f32 = jnp.bfloat16, jnp.float32
VMEM = pl.BlockSpec(memory_space=pltpu.VMEM)
STAY = pl.BlockSpec(memory_space=pl.ANY)
AXES = ("tok", "slot", "hid")


def call(body, outs, *args, name, flops=0, nbytes=0, stay=0, scratch=()):
    return pl.pallas_call(
        body,
        out_shape=[jax.ShapeDtypeStruct(s, d) for s, d in outs],
        in_specs=[VMEM] * (len(args) - stay) + [STAY] * stay,
        out_specs=[VMEM] * len(outs),
        scratch_shapes=list(scratch),
        name=name,
        compiler_params=pltpu.CompilerParams(vmem_limit_bytes=24 * 2**20),
        cost_estimate=pl.CostEstimate(flops=flops, bytes_accessed=nbytes, transcendentals=0),
    )(*args)


def swap(value, axis, step):
    return lax.ppermute(value, axis, [(i, i ^ step) for i in range(lax.axis_size(axis))])


def swap_by_core(value, moves):
    rows, blocks = lax.axis_size("tok"), lax.axis_size("slot")
    pairs = []
    for row in range(rows):
        for block in range(blocks):
            for core, move in enumerate(moves):
                if move is None:
                    continue
                axis, step = move
                to_row = row ^ step if axis == "tok" else row
                to_block = block ^ step if axis == "slot" else block
                pairs.append(((row * blocks + block) * 2 + core, (to_row * blocks + to_block) * 2 + core))
    return lax.ppermute(value, AXES, pairs)


def halves(half):
    core = lax.axis_index("hid")
    mine = pl.ds(pl.multiple_of(core * half, half), half)
    other = pl.ds(pl.multiple_of((1 - core) * half, half), half)
    return mine, other


def total_at(slots, half, at):
    return slice(slots + 8 * (at // half), slots + 8 * (at // half) + 8)


def weigh(tok_ref, key_ref, key_scale):
    width = tok_ref.shape[1]
    tok = tok_ref[...].astype(f32)
    tok_scale = lax.rsqrt(jnp.sum(tok * tok, axis=1, keepdims=True) / width + epsilon)
    logits = jnp.dot(tok_ref[...], key_ref[...], preferred_element_type=f32)
    return jnp.exp(logits * (tok_scale * (4.0 / width)) * key_scale)


def collect(tok_ref, weights, half):
    low = weights.astype(bf16)
    mine, other = halves(half)
    dims = (((0,), (0,)), ((), ()))
    keep = lax.dot_general(low, tok_ref[:, mine], dims, preferred_element_type=f32)
    send = lax.dot_general(low, tok_ref[:, other], dims, preferred_element_type=f32)
    total = jnp.broadcast_to(jnp.sum(weights, axis=0, keepdims=True), (8, weights.shape[1]))
    return low, keep, send, total


def dispatch_own_body(half, tok_ref, key_ref, in_ref, out_ref, low_ref, keep_ref, send_ref, scale_ref, keys_ref, in_here, out_here, sems):
    copies = [pltpu.make_async_copy(in_ref, in_here, sems.at[0]), pltpu.make_async_copy(out_ref, out_here, sems.at[1])]
    for copy in copies:
        copy.start()
    width, slots = key_ref.shape
    key = key_ref[...].astype(f32)
    key_scale = lax.rsqrt(jnp.sum(key * key, axis=0, keepdims=True) / width + epsilon)
    scale_ref[...] = jnp.broadcast_to(key_scale, (8, slots))
    keys_ref[...] = key_ref[...]
    low, keep, send, total = collect(tok_ref, weigh(tok_ref, key_ref, key_scale), half)
    low_ref[...] = low
    keep_ref[0:slots, :] = keep
    send_ref[0:slots, :] = send
    for at in range(0, slots, half):
        wide = min(half, slots - at)
        for ref in (keep_ref, send_ref):
            ref[total_at(slots, half, at), 0:wide] = total[:, at : at + wide]
    for copy in copies:
        copy.wait()


def dispatch_other_body(half, tok_ref, key_ref, scale_ref, keep_in, send_in, low_ref, keep_ref, send_ref):
    slots = key_ref.shape[1]
    low, keep, send, total = collect(tok_ref, weigh(tok_ref, key_ref, scale_ref[0:1, :]), half)
    low_ref[...] = low
    keep_ref[0:slots, :] = keep + keep_in[0:slots, :]
    send_ref[0:slots, :] = send + send_in[0:slots, :]
    for at in range(0, slots, half):
        wide = min(half, slots - at)
        place = total_at(slots, half, at)
        for ref, old in ((keep_ref, keep_in), (send_ref, send_in)):
            ref[place, 0:wide] = total[:, at : at + wide] + old[place, 0:wide]


def total_rows(slots, half):
    return 8 * pl.cdiv(3 * pl.cdiv(slots, half), 8)


def share_body(owned, slots, keep_ref, recv_ref, mine_ref, total_ref, *send_refs):
    half = keep_ref.shape[1]
    row = lax.axis_index("tok")
    terms = []
    for at in range(0, slots, half):
        wide = min(half, slots - at)
        place = total_at(slots, half, at)
        total = keep_ref[place, 0:wide] + recv_ref[place, 0:wide]
        total_ref[:, at : at + wide] = total
        total = total[0:1, :]
        for _ in range(3):
            term = total.astype(bf16)
            terms.append((wide, term))
            total = total - term.astype(f32)
    for step in range(slots // owned):
        start = pl.ds(pl.multiple_of((row ^ step) * owned, owned), owned)
        piece = keep_ref[start, :] + recv_ref[start, :]
        if step == 0:
            mine_ref[...] = piece
            continue
        ref = send_refs[step - 1]
        ref[0:owned, :] = piece.astype(bf16)
        ref[owned:, :] = jnp.zeros((ref.shape[0] - owned, half), bf16)
        for index, (wide, term) in enumerate(terms):
            ref[owned + index : owned + index + 1, 0:wide] = term


def inputs_body(mine_ref, total_ref, *refs):
    piece_refs, out_ref = refs[:-1], refs[-1]
    owned, half = mine_ref.shape
    slots = total_ref.shape[1]
    numer = mine_ref[...]
    denom = jnp.zeros((owned, 1), f32)
    for ref in piece_refs:
        numer = numer + ref[0:owned, :].astype(f32)
    for at in range(0, slots, half):
        wide = min(half, slots - at)
        total = total_ref[0:1, at : at + wide]
        first = owned + 3 * (at // half)
        for ref in piece_refs:
            for index in range(first, first + 3):
                total = total + ref[index : index + 1, 0:wide].astype(f32)
        lane = lax.broadcasted_iota(jnp.int32, (owned, wide), 1) + at
        wanted = lax.broadcasted_iota(jnp.int32, (owned, wide), 0) + lax.axis_index("tok") * owned
        total = jnp.where(lane == wanted, jnp.broadcast_to(total, (owned, wide)), 0.0)
        denom = denom + jnp.sum(total, axis=1, keepdims=True)
    out_ref[...] = (numer / denom).astype(bf16)


def expert_body(mine_ref, other_ref, in_ref, out_w_ref, out_ref):
    mine, other = halves(mine_ref.shape[1])
    value = jnp.dot(mine_ref[...], in_ref[mine, :], preferred_element_type=f32)
    value = value + jnp.dot(other_ref[...], in_ref[other, :], preferred_element_type=f32)
    hidden = jax.nn.gelu(value, approximate=True).astype(bf16)
    out_ref[...] = jnp.dot(hidden, out_w_ref[...], preferred_element_type=f32)


def outputs_body(part_ref, recv_ref, full_ref):
    full_ref[...] = (part_ref[...] + recv_ref[...]).astype(bf16)


def combine_body(blocks, rows, slots, plan, *refs):
    low_refs, full_ref, pieces = refs[:blocks], refs[blocks], refs[blocks + 1 : -2]
    out_ref, all_ref = refs[-2], refs[-1]
    owned = full_ref.shape[0]
    core = lax.axis_index("hid")
    row = lax.axis_index("tok")

    def put(step, ref):
        block, expert = step
        start = block * slots + (row ^ expert) * owned
        all_ref[pl.ds(pl.multiple_of(start, owned), owned), :] = ref[...]

    put((0, 0), full_ref)
    for index, steps in enumerate(plan):
        for turn in range(2):
            ref = pieces[2 * index + turn]
            for holder in range(2):
                step = steps[holder ^ turn]
                if step is not None:
                    pl.when(core == holder)(functools.partial(put, step, ref))
    numer = None
    denom = None
    for block in range(blocks):
        low = low_refs[block][...]
        part = jnp.dot(low, all_ref[block * slots : (block + 1) * slots, :], preferred_element_type=f32)
        total = jnp.sum(low.astype(f32), axis=1, keepdims=True)
        numer = part if numer is None else numer + part
        denom = total if denom is None else denom + total
    out_ref[...] = numer / denom


def local(tokens, slot_keys, w_in, w_out):
    count, width = tokens.shape
    slots = slot_keys.shape[1]
    hidden = w_in.shape[3]
    rows, blocks = lax.axis_size("tok"), lax.axis_size("slot")
    owned = slots // rows
    half = width // 2
    extra = 8 * pl.cdiv(slots, half)
    part = ((slots + extra, half), f32)
    mac = 4 * count * width * slots

    arrived = [swap(tokens, "slot", step) for step in range(1, blocks)]
    low, keep, send, scale, keys, in_here, out_here = call(
        functools.partial(dispatch_own_body, half),
        [((count, slots), bf16), part, part, ((8, slots), f32), ((width, slots), bf16), ((width, hidden), bf16), ((hidden, width), bf16)],
        tokens, slot_keys, w_in[0, 0], w_out[0, 0],
        name="dispatch_own", flops=mac, nbytes=8 * hidden * width, stay=2, scratch=[pltpu.SemaphoreType.DMA((2,))],
    )
    lows = [low]
    for step in range(1, blocks):
        low, keep, send = call(
            functools.partial(dispatch_other_body, half),
            [((count, slots), bf16), part, part],
            arrived[step - 1], keys, scale, keep, send, name="dispatch_other", flops=mac, nbytes=2 * count * width,
        )
        lows.append(low)
    recv = swap(send, "hid", 1)
    mine, total, *sends = call(
        functools.partial(share_body, owned, slots),
        [((owned, half), f32), ((8, slots), f32)] + [((owned + total_rows(slots, half), half), bf16)] * (rows - 1),
        keep, recv, name="share", nbytes=12 * slots * half,
    )
    pieces = [swap(sends[step - 1], "tok", step) for step in range(1, rows)]
    lows = lows[:1] + [swap(lows[step], "slot", step) for step in range(1, blocks)]
    pieces, lows = lax.optimization_barrier((pieces, lows))
    (inputs,) = call(
        inputs_body, [((owned, half), bf16)],
        mine, total, *pieces, name="slot_inputs", nbytes=8 * owned * width,
    )
    inputs_other = swap(inputs, "hid", 1)
    (outputs_part,) = call(
        expert_body, [((owned, width), f32)],
        inputs, inputs_other, in_here, out_here,
        name="expert", flops=4 * owned * width * hidden, nbytes=4 * width * hidden,
    )
    outputs_recv = swap(outputs_part, "hid", 1)
    (full,) = call(outputs_body, [((owned, width), bf16)], outputs_part, outputs_recv, name="slot_outputs", nbytes=8 * owned * width)

    moves = [("tok", step) for step in range(1, rows)] + [("slot", step) for step in range(1, blocks)]
    moves += [None] * (len(moves) % 2)
    flights, plan = [], []
    turns = [moves[at : at + 2] for at in range(0, len(moves), 2)][::-1]
    for turn in turns:
        got = swap_by_core(full, turn)
        flights.append(got)
        plan.append([move and ((0, move[1]) if move[0] == "tok" else (move[1], 0)) for move in turn])
    for at, turn in list(enumerate(turns)):
        for step in range(1, blocks):
            along = [("slot", step) if move and move[0] == "tok" else None for move in turn]
            if any(along):
                flights.append(swap_by_core(flights[at], along))
                plan.append([move and (step, turn[core][1]) for core, move in enumerate(along)])
    pairs = []
    for got, steps in zip(flights, plan):
        pairs += [got, swap(got, "hid", 1)]
    return pl.pallas_call(
        functools.partial(combine_body, blocks, rows, slots, plan),
        out_shape=jax.ShapeDtypeStruct((count, width), f32),
        in_specs=[VMEM] * (blocks + 1 + len(pairs)),
        out_specs=VMEM,
        scratch_shapes=[pltpu.VMEM((blocks * slots, width), bf16)],
        name="combine",
        compiler_params=pltpu.CompilerParams(vmem_limit_bytes=40 * 2**20),
    )(*lows, full, *pairs)


def solution(mesh):
    in_specs = (
        P(("groups", "tok", "slot", "hid"), None),
        P("groups", "slot"),
        P(("groups", "slot"), "tok", None, "hid"),
        P(("groups", "slot"), "tok", "hid", None),
    )
    out_specs = P(("groups", "tok", "slot", "hid"), None)
    return jax.shard_map(local, mesh=mesh, in_specs=in_specs, out_specs=out_specs, check_vma=False)
```

```python
import functools

import jax
import jax.numpy as jnp
from jax import lax
from jax.experimental import pallas as pl
from jax.experimental.pallas import tpu as pltpu
from jax.sharding import PartitionSpec as P

epsilon = 1e-06
bf16, f32 = jnp.bfloat16, jnp.float32
VMEM = pl.BlockSpec(memory_space=pltpu.VMEM)
STAY = pl.BlockSpec(memory_space=pl.ANY)
AXES = ("tok", "slot", "hid")


def call(body, outs, *args, name, flops=0, nbytes=0, stay=0, scratch=()):
    return pl.pallas_call(
        body,
        out_shape=[jax.ShapeDtypeStruct(s, d) for s, d in outs],
        in_specs=[VMEM] * (len(args) - stay) + [STAY] * stay,
        out_specs=[VMEM] * len(outs),
        scratch_shapes=list(scratch),
        name=name,
        compiler_params=pltpu.CompilerParams(vmem_limit_bytes=24 * 2**20),
        cost_estimate=pl.CostEstimate(flops=flops, bytes_accessed=nbytes, transcendentals=0),
    )(*args)


def swap(value, axis, step):
    return lax.ppermute(value, axis, [(i, i ^ step) for i in range(lax.axis_size(axis))])


def swap_by_core(value, moves):
    rows, blocks = lax.axis_size("tok"), lax.axis_size("slot")
    pairs = []
    for row in range(rows):
        for block in range(blocks):
            for core, (over, across) in enumerate(moves):
                to = (row ^ over) * blocks + (block ^ across)
                pairs.append(((row * blocks + block) * 2 + core, to * 2 + core))
    return lax.ppermute(value, AXES, pairs)


def halves(half):
    core = lax.axis_index("hid")
    mine = pl.ds(pl.multiple_of(core * half, half), half)
    other = pl.ds(pl.multiple_of((1 - core) * half, half), half)
    return mine, other


def total_at(slots, half, at):
    return slice(slots + 8 * (at // half), slots + 8 * (at // half) + 8)


def weigh(tok_ref, key_ref, key_scale):
    width = tok_ref.shape[1]
    tok = tok_ref[...].astype(f32)
    tok_scale = lax.rsqrt(jnp.sum(tok * tok, axis=1, keepdims=True) / width + epsilon)
    logits = jnp.dot(tok_ref[...], key_ref[...], preferred_element_type=f32)
    return jnp.exp(logits * (tok_scale * (4.0 / width)) * key_scale)


def collect(tok_ref, weights, half):
    low = weights.astype(bf16)
    mine, other = halves(half)
    dims = (((0,), (0,)), ((), ()))
    keep = lax.dot_general(low, tok_ref[:, mine], dims, preferred_element_type=f32)
    send = lax.dot_general(low, tok_ref[:, other], dims, preferred_element_type=f32)
    total = jnp.broadcast_to(jnp.sum(weights, axis=0, keepdims=True), (8, weights.shape[1]))
    return low, keep, send, total


def dispatch_own_body(half, tok_ref, key_ref, in_ref, out_ref, low_ref, keep_ref, send_ref, scale_ref, keys_ref, in_here, out_here, sems):
    copies = [pltpu.make_async_copy(in_ref, in_here, sems.at[0]), pltpu.make_async_copy(out_ref, out_here, sems.at[1])]
    for copy in copies:
        copy.start()
    width, slots = key_ref.shape
    key = key_ref[...].astype(f32)
    key_scale = lax.rsqrt(jnp.sum(key * key, axis=0, keepdims=True) / width + epsilon)
    scale_ref[...] = jnp.broadcast_to(key_scale, (8, slots))
    keys_ref[...] = key_ref[...]
    low, keep, send, total = collect(tok_ref, weigh(tok_ref, key_ref, key_scale), half)
    low_ref[...] = low
    keep_ref[0:slots, :] = keep
    send_ref[0:slots, :] = send
    for at in range(0, slots, half):
        wide = min(half, slots - at)
        for ref in (keep_ref, send_ref):
            ref[total_at(slots, half, at), 0:wide] = total[:, at : at + wide]
    for copy in copies:
        copy.wait()


def dispatch_other_body(half, tok_ref, key_ref, scale_ref, keep_in, send_in, low_ref, keep_ref, send_ref):
    slots = key_ref.shape[1]
    low, keep, send, total = collect(tok_ref, weigh(tok_ref, key_ref, scale_ref[0:1, :]), half)
    low_ref[...] = low
    keep_ref[0:slots, :] = keep + keep_in[0:slots, :]
    send_ref[0:slots, :] = send + send_in[0:slots, :]
    for at in range(0, slots, half):
        wide = min(half, slots - at)
        place = total_at(slots, half, at)
        for ref, old in ((keep_ref, keep_in), (send_ref, send_in)):
            ref[place, 0:wide] = total[:, at : at + wide] + old[place, 0:wide]


def total_rows(slots, half):
    return 8 * pl.cdiv(3 * pl.cdiv(slots, half), 8)


def share_body(owned, slots, keep_ref, recv_ref, mine_ref, total_ref, *send_refs):
    half = keep_ref.shape[1]
    row = lax.axis_index("tok")
    terms = []
    for at in range(0, slots, half):
        wide = min(half, slots - at)
        place = total_at(slots, half, at)
        total = keep_ref[place, 0:wide] + recv_ref[place, 0:wide]
        total_ref[:, at : at + wide] = total
        total = total[0:1, :]
        for _ in range(3):
            term = total.astype(bf16)
            terms.append((wide, term))
            total = total - term.astype(f32)
    for step in range(slots // owned):
        start = pl.ds(pl.multiple_of((row ^ step) * owned, owned), owned)
        piece = keep_ref[start, :] + recv_ref[start, :]
        if step == 0:
            mine_ref[...] = piece
            continue
        ref = send_refs[step - 1]
        ref[0:owned, :] = piece.astype(bf16)
        ref[owned:, :] = jnp.zeros((ref.shape[0] - owned, half), bf16)
        for index, (wide, term) in enumerate(terms):
            ref[owned + index : owned + index + 1, 0:wide] = term


def inputs_body(mine_ref, total_ref, *refs):
    piece_refs, out_ref = refs[:-1], refs[-1]
    owned, half = mine_ref.shape
    slots = total_ref.shape[1]
    numer = mine_ref[...]
    denom = jnp.zeros((owned, 1), f32)
    for ref in piece_refs:
        numer = numer + ref[0:owned, :].astype(f32)
    for at in range(0, slots, half):
        wide = min(half, slots - at)
        total = total_ref[0:1, at : at + wide]
        first = owned + 3 * (at // half)
        for ref in piece_refs:
            for index in range(first, first + 3):
                total = total + ref[index : index + 1, 0:wide].astype(f32)
        lane = lax.broadcasted_iota(jnp.int32, (owned, wide), 1) + at
        wanted = lax.broadcasted_iota(jnp.int32, (owned, wide), 0) + lax.axis_index("tok") * owned
        total = jnp.where(lane == wanted, jnp.broadcast_to(total, (owned, wide)), 0.0)
        denom = denom + jnp.sum(total, axis=1, keepdims=True)
    out_ref[...] = (numer / denom).astype(bf16)


def expert_first_body(mine_ref, in_ref, value_ref):
    mine, _ = halves(mine_ref.shape[1])
    value_ref[...] = jnp.dot(mine_ref[...], in_ref[mine, :], preferred_element_type=f32)


def expert_body(value_ref, other_ref, in_ref, out_w_ref, out_ref):
    _, other = halves(other_ref.shape[1])
    value = value_ref[...] + jnp.dot(other_ref[...], in_ref[other, :], preferred_element_type=f32)
    hidden = jax.nn.gelu(value, approximate=True).astype(bf16)
    out_ref[...] = jnp.dot(hidden, out_w_ref[...], preferred_element_type=f32)


def outputs_body(part_ref, recv_ref, full_ref):
    full_ref[...] = (part_ref[...] + recv_ref[...]).astype(bf16)


def gather_pieces(all_ref, pieces, plan, slots, owned, first):
    core = lax.axis_index("hid")
    row = lax.axis_index("tok")
    pieces = list(pieces)

    def put(ref, starts, turn):
        start = jnp.where(core == turn, starts[0], starts[1])
        all_ref[pl.ds(pl.multiple_of(start, owned), owned), :] = ref[...]

    for moves in plan:
        starts = [(across - first) * slots + (row ^ over) * owned for over, across in moves]
        put(pieces.pop(0), starts, 0)
        if moves[0] != moves[1]:
            put(pieces.pop(0), starts, 1)


def combine_first_body(blocks, slots, plan, *refs):
    low_refs, full_ref, pieces = refs[:blocks], refs[blocks], refs[blocks + 1 : -3]
    numer_ref, denom_ref, all_ref = refs[-3:]
    owned = full_ref.shape[0]
    all_ref[...] = jnp.zeros_like(all_ref)
    gather_pieces(all_ref, (full_ref,) + pieces, [((0, 0), (0, 0))] + plan, slots, owned, 0)
    numer = None
    denom = None
    for block in range(blocks):
        low = low_refs[block][...]
        part = jnp.dot(low, all_ref[block * slots : (block + 1) * slots, :], preferred_element_type=f32)
        total = jnp.sum(low.astype(f32), axis=1, keepdims=True)
        numer = part if numer is None else numer + part
        denom = total if denom is None else denom + total
    numer_ref[...] = numer
    denom_ref[...] = jnp.broadcast_to(denom, denom_ref.shape)


def combine_last_body(blocks, slots, owned, plan, *refs):
    low_refs, numer_ref, denom_ref, pieces = refs[: blocks - 1], refs[blocks - 1], refs[blocks], refs[blocks + 1 : -2]
    out_ref, all_ref = refs[-2:]

    @pl.when(pl.program_id(0) == 0)
    def _():
        all_ref[...] = jnp.zeros_like(all_ref)
        gather_pieces(all_ref, pieces, plan, slots, owned, 1)

    numer = numer_ref[...]
    for block in range(blocks - 1):
        numer = numer + jnp.dot(low_refs[block][...], all_ref[block * slots : (block + 1) * slots, :], preferred_element_type=f32)
    out_ref[...] = numer / denom_ref[:, 0:1]


def local(tokens, slot_keys, w_in, w_out):
    count, width = tokens.shape
    slots = slot_keys.shape[1]
    hidden = w_in.shape[3]
    rows, blocks = lax.axis_size("tok"), lax.axis_size("slot")
    owned = slots // rows
    half = width // 2
    extra = 8 * pl.cdiv(slots, half)
    part = ((slots + extra, half), f32)
    mac = 4 * count * width * slots

    arrived = [swap(tokens, "slot", step) for step in range(1, blocks)]
    low, keep, send, scale, keys, in_here, out_here = call(
        functools.partial(dispatch_own_body, half),
        [((count, slots), bf16), part, part, ((8, slots), f32), ((width, slots), bf16), ((width, hidden), bf16), ((hidden, width), bf16)],
        tokens, slot_keys, w_in[0, 0], w_out[0, 0],
        name="dispatch_own", flops=mac, nbytes=8 * hidden * width, stay=2, scratch=[pltpu.SemaphoreType.DMA((2,))],
    )
    lows = [low]
    for step in range(1, blocks):
        low, keep, send = call(
            functools.partial(dispatch_other_body, half),
            [((count, slots), bf16), part, part],
            arrived[step - 1], keys, scale, keep, send, name="dispatch_other", flops=mac, nbytes=2 * count * width,
        )
        lows.append(low)
    recv = swap(send, "hid", 1)
    mine, total, *sends = call(
        functools.partial(share_body, owned, slots),
        [((owned, half), f32), ((8, slots), f32)] + [((owned + total_rows(slots, half), half), bf16)] * (rows - 1),
        keep, recv, name="share", nbytes=12 * slots * half,
    )
    pieces = [swap(sends[step - 1], "tok", step) for step in range(1, rows)]
    lows = lows[:1] + [swap(lows[step], "slot", step) for step in range(1, blocks)]
    pieces, lows = lax.optimization_barrier((pieces, lows))
    (inputs,) = call(
        inputs_body, [((owned, half), bf16)],
        mine, total, *pieces, name="slot_inputs", nbytes=8 * owned * width,
    )
    inputs_other = swap(inputs, "hid", 1)
    (value,) = call(
        expert_first_body, [((owned, hidden), f32)], inputs, in_here,
        name="expert_first", flops=owned * width * hidden, nbytes=width * hidden,
    )
    (outputs_part,) = call(
        expert_body, [((owned, width), f32)],
        value, inputs_other, in_here, out_here,
        name="expert", flops=4 * owned * width * hidden, nbytes=4 * width * hidden,
    )
    outputs_recv = swap(outputs_part, "hid", 1)
    (full,) = call(
        outputs_body, [((owned, width), bf16)],
        outputs_part, outputs_recv, name="slot_outputs", nbytes=8 * owned * width,
    )

    far = [(over, 0) for over in range(2, rows)]
    near = [(1, 0)] + [(0, across) for across in range(1, blocks)]
    flights = []

    def fly(value, moves, came=None):
        came = came or moves
        flights.append((swap_by_core(value, moves), came))
        return flights[-1][0]

    passed = []
    for at in range(0, len(far), 2):
        moves = far[at : at + 2]
        got = fly(full, moves)
        passed += [(got, moves)]
    for at in range(0, len(near), 2):
        fly(full, near[at : at + 2])
    for across in range(1, blocks):
        fly(full, [(1, across)] * 2)
    direct = len(flights)
    held = lax.optimization_barrier([got for got, _ in passed] + [got for got, came in flights if came[0] == came[1]])
    passed = [(got, moves) for got, (_, moves) in zip(held, passed)]
    for got, moves in passed:
        for across in range(1, blocks):
            fly(got, [(0, across)] * 2, [(over, across) for over, _ in moves])
    def both(flights):
        pieces = []
        for got, came in flights:
            pieces += [got] if came[0] == came[1] else [got, swap(got, "hid", 1)]
        return pieces, [came for _, came in flights]

    pieces, plan = both(flights[:direct])
    numer, denom = call(
        functools.partial(combine_first_body, blocks, slots, plan),
        [((count, width), f32), ((count, 128), f32)],
        *lows, full, *pieces,
        name="combine_first", flops=2 * count * width * slots * blocks, nbytes=8 * count * width,
        scratch=[pltpu.VMEM((blocks * slots, width), bf16)],
    )
    pieces, plan = both(flights[direct:])
    tile = count // 2
    return pl.pallas_call(
        functools.partial(combine_last_body, blocks, slots, owned, plan),
        out_shape=jax.ShapeDtypeStruct((count, width), f32),
        grid=(count // tile,),
        in_specs=[pl.BlockSpec((tile, slots), lambda i: (i, 0))] * (blocks - 1)
        + [pl.BlockSpec((tile, width), lambda i: (i, 0)), pl.BlockSpec((tile, 128), lambda i: (i, 0))]
        + [VMEM] * len(pieces),
        out_specs=pl.BlockSpec((tile, width), lambda i: (i, 0)),
        scratch_shapes=[pltpu.VMEM(((blocks - 1) * slots, width), bf16)],
        name="combine_last",
        compiler_params=pltpu.CompilerParams(vmem_limit_bytes=24 * 2**20),
    )(*lows[1:], numer, denom, *pieces)


def solution(mesh):
    in_specs = (
        P(("groups", "tok", "slot", "hid"), None),
        P("groups", "slot"),
        P(("groups", "slot"), "tok", None, "hid"),
        P(("groups", "slot"), "tok", "hid", None),
    )
    out_specs = P(("groups", "tok", "slot", "hid"), None)
    return jax.shard_map(local, mesh=mesh, in_specs=in_specs, out_specs=out_specs, check_vma=False)
```

```python
import functools

import jax
import jax.numpy as jnp
from jax import lax
from jax.experimental import pallas as pl
from jax.experimental.pallas import tpu as pltpu
from jax.sharding import PartitionSpec as P

epsilon = 1e-06
bf16, f32 = jnp.bfloat16, jnp.float32
VMEM = pl.BlockSpec(memory_space=pltpu.VMEM)
STAY = pl.BlockSpec(memory_space=pltpu.HBM)
AXES = ("tok", "slot", "hid")


def call(body, outs, *args, name, flops=0, nbytes=0, stay=0, scratch=()):
    return pl.pallas_call(
        body,
        out_shape=[jax.ShapeDtypeStruct(s, d) for s, d in outs],
        in_specs=[VMEM] * (len(args) - stay) + [STAY] * stay,
        out_specs=[VMEM] * len(outs),
        scratch_shapes=list(scratch),
        name=name,
        compiler_params=pltpu.CompilerParams(vmem_limit_bytes=24 * 2**20),
        cost_estimate=pl.CostEstimate(flops=flops, bytes_accessed=nbytes, transcendentals=0),
    )(*args)


def swap(value, axis, step):
    return lax.ppermute(value, axis, [(i, i ^ step) for i in range(lax.axis_size(axis))])


def swap_by_core(value, moves):
    rows, blocks = lax.axis_size("tok"), lax.axis_size("slot")
    pairs = []
    for row in range(rows):
        for block in range(blocks):
            for core, (over, across) in enumerate(moves):
                to = (row ^ over) * blocks + (block ^ across)
                pairs.append(((row * blocks + block) * 2 + core, to * 2 + core))
    return lax.ppermute(value, AXES, pairs)


def spread(value, step, across):
    rows, blocks = lax.axis_size("tok"), lax.axis_size("slot")
    per = rows // 2
    pairs = []
    for row in range(rows):
        for block in range(blocks):
            for core in range(2):
                to = (core * per + (row % per ^ step)) * blocks + (block ^ across)
                pairs.append(((row * blocks + block) * 2 + core, to * 2 + (row // per ^ core)))
    return lax.ppermute(value, AXES, pairs)


def keys_body(key_ref, out_ref, sem):
    part = out_ref.shape[1]
    core = lax.axis_index("hid")
    copy = pltpu.make_async_copy(key_ref.at[:, pl.ds(pl.multiple_of(core * part, part), part)], out_ref, sem)
    copy.start()
    copy.wait()


def stage_body(after_ref, from_ref, here_ref, sem):
    copy = pltpu.make_async_copy(from_ref, here_ref, sem)
    copy.start()
    copy.wait()


def stage(after, value):
    return call(stage_body, [(value.shape, value.dtype)], after, value, name="stage", nbytes=4 * value.size, stay=1, scratch=[pltpu.SemaphoreType.DMA])[0]


def dispatch_body(first, owned, *refs):
    if first:
        tok_refs, key_ref, low_refs, scale_refs, piece_refs, numer_ref = refs[0:2], refs[2], refs[3:5], refs[5:7], refs[8:-1], refs[-1]
        refs[7][...] = tok_refs[0][...]
    else:
        tok_refs, key_ref, scale_refs, low_refs, piece_refs, numer_ref = refs[0:2], refs[2], refs[3:5], refs[5:7], refs[7:-1], refs[-1]
    width, part = key_ref.shape
    key = key_ref[...].astype(f32)
    key_scale = lax.rsqrt(jnp.sum(key * key, axis=0, keepdims=True) / width + epsilon)
    numer = None
    total = None
    for tok_ref, low_ref, scale_ref in zip(tok_refs, low_refs, scale_refs):
        if first:
            tok = tok_ref[...].astype(f32)
            scale = lax.rsqrt(jnp.sum(tok * tok, axis=1, keepdims=True) / width + epsilon) * (4.0 / width)
            scale_ref[...] = jnp.broadcast_to(scale, scale_ref.shape)
        else:
            scale = scale_ref[:, 0:1]
        logits = jnp.dot(tok_ref[...], key_ref[...], preferred_element_type=f32)
        weights = jnp.exp(logits * scale * key_scale)
        low = weights.astype(bf16)
        low_ref[...] = low
        mine = lax.dot_general(low, tok_ref[...], (((0,), (0,)), ((), ())), preferred_element_type=f32)
        numer = mine if numer is None else numer + mine
        mine = jnp.sum(weights, axis=0, keepdims=True)
        total = mine if total is None else total + mine
    numer_ref[...] = numer
    terms = []
    for _ in range(3):
        term = total.astype(bf16)
        terms.append(term)
        total = total - term.astype(f32)
    per = part // owned
    low_row = lax.rem(lax.axis_index("tok"), per)
    for step, ref in enumerate(piece_refs):
        start = pl.multiple_of((low_row ^ step) * owned, owned)
        ref[0:owned, :] = numer_ref[pl.ds(start, owned), :].astype(bf16)
        ref[owned:, :] = jnp.zeros((8, width), bf16)
        for index, term in enumerate(terms):
            ref[owned + index : owned + index + 1, 0:part] = term


def sum_body(*refs):
    piece_refs, out_ref = refs[:-1], refs[-1]
    out = None
    for ref in piece_refs:
        piece = ref[...].astype(f32)
        out = piece if out is None else out + piece
    out_ref[...] = out


def expert_body(part, mine_ref, other_ref, in_ref, out_w_ref, out_ref):
    owned = out_ref.shape[0]
    numer = mine_ref[0:owned, :] + other_ref[0:owned, :]
    total = mine_ref[owned:, 0:part] + other_ref[owned:, 0:part]
    total = total[0:1, :] + total[1:2, :] + total[2:3, :]
    per = part // owned
    lane = lax.broadcasted_iota(jnp.int32, (owned, part), 1)
    wanted = lax.broadcasted_iota(jnp.int32, (owned, part), 0) + lax.rem(lax.axis_index("tok"), per) * owned
    denom = jnp.sum(jnp.where(lane == wanted, jnp.broadcast_to(total, (owned, part)), 0.0), axis=1, keepdims=True)
    inputs = (numer / denom).astype(bf16)
    value = jnp.dot(inputs, in_ref[...], preferred_element_type=f32)
    hidden = jax.nn.gelu(value, approximate=True).astype(bf16)
    out_ref[...] = jnp.dot(hidden, out_w_ref[...], preferred_element_type=f32)


def outputs_body(part_ref, recv_ref, full_ref):
    full_ref[...] = (part_ref[...] + recv_ref[...]).astype(bf16)


def gather_pieces(all_ref, pieces, plan, slots, owned, first):
    core = lax.axis_index("hid")
    row = lax.axis_index("tok")
    pieces = list(pieces)

    def put(ref, starts, turn):
        start = jnp.where(core == turn, starts[0], starts[1])
        all_ref[pl.ds(pl.multiple_of(start, owned), owned), :] = ref[...]

    for moves in plan:
        starts = [(across - first) * slots + (row ^ over) * owned for over, across in moves]
        put(pieces.pop(0), starts, 0)
        if moves[0] != moves[1]:
            put(pieces.pop(0), starts, 1)


def mix(low_refs, all_ref, blocks, slots):
    part = slots // 2
    core = lax.axis_index("hid")
    numer = None
    for index, ref in enumerate(low_refs):
        start = (index // 2) * slots + (core if index % 2 == 0 else 1 - core) * part
        mine = jnp.dot(ref[...], all_ref[pl.ds(pl.multiple_of(start, part), part), :], preferred_element_type=f32)
        numer = mine if numer is None else numer + mine
    return numer


def combine_first_body(blocks, slots, plan, *refs):
    low_refs, full_ref, pieces = refs[: 2 * blocks], refs[2 * blocks], refs[2 * blocks + 1 : -3]
    numer_ref, denom_ref, all_ref = refs[-3:]
    all_ref[...] = jnp.zeros_like(all_ref)
    gather_pieces(all_ref, (full_ref,) + pieces, [((0, 0), (0, 0))] + plan, slots, full_ref.shape[0], 0)
    numer_ref[...] = mix(low_refs, all_ref, blocks, slots)
    denom = None
    for ref in low_refs:
        total = jnp.sum(ref[...].astype(f32), axis=1, keepdims=True)
        denom = total if denom is None else denom + total
    denom_ref[...] = jnp.broadcast_to(denom, denom_ref.shape)


def combine_last_body(blocks, slots, owned, plan, *refs):
    lows = 2 * (blocks - 1)
    low_refs, numer_ref, denom_ref, pieces = refs[:lows], refs[lows], refs[lows + 1], refs[lows + 2 : -2]
    out_ref, all_ref = refs[-2:]

    @pl.when(pl.program_id(0) == 0)
    def _():
        all_ref[...] = jnp.zeros_like(all_ref)
        gather_pieces(all_ref, pieces, plan, slots, owned, 1)

    out_ref[...] = (numer_ref[...] + mix(low_refs, all_ref, blocks - 1, slots)) / denom_ref[:, 0:1]


def local(tokens, slot_keys, w_in, w_out):
    count, width = tokens.shape
    slots = slot_keys.shape[1]
    hidden = w_in.shape[3]
    rows, blocks = lax.axis_size("tok"), lax.axis_size("slot")
    owned = slots // rows
    part = slots // 2
    mac = 8 * count * width * part
    piece = ((owned + 8, width), bf16)
    lows_shape = [((count, part), bf16)] * 2
    scratch = [pltpu.VMEM((part, width), f32)]

    (keys,) = call(keys_body, [((width, part), bf16)], slot_keys, name="keys", nbytes=4 * width * part, stay=1, scratch=[pltpu.SemaphoreType.DMA])
    arrived = [swap(keys, "slot", across) for across in range(1, blocks)]
    beside = swap(tokens, "hid", 1)
    low_mine, low_send, scale, scale_beside, here, *pieces = call(
        functools.partial(dispatch_body, True, owned),
        lows_shape + [((count, 128), f32)] * 2 + [((count, width), bf16)] + [piece] * (rows // 2),
        tokens, beside, keys, name="dispatch_own", flops=mac, nbytes=4 * count * width, scratch=scratch,
    )
    sent = [spread(value, step, 0) for step, value in enumerate(pieces)]
    lows = [low_mine, swap(low_send, "hid", 1)]
    for across in range(1, blocks):
        low_mine, low_send, *pieces = call(
            functools.partial(dispatch_body, False, owned),
            lows_shape + [piece] * (rows // 2),
            here, beside, arrived[across - 1], scale, scale_beside,
            name="dispatch_other", flops=mac, nbytes=4 * count * width, scratch=scratch,
        )
        sent += [spread(value, step, across) for step, value in enumerate(pieces)]
        lows += [low_mine, swap(low_send, "hid", 1)]
    out_here = stage(low_send, w_out[0, 0])
    sent, lows, out_here = lax.optimization_barrier((sent, lows, out_here))
    (mine,) = call(sum_body, [((owned + 8, width), f32)], *sent, name="sum_pieces", nbytes=4 * owned * width * len(sent))
    other = swap(mine, "hid", 1)
    (outputs_part,) = call(
        functools.partial(expert_body, part), [((owned, width), f32)],
        mine, other, w_in[0, 0], out_here,
        name="expert", flops=4 * owned * width * hidden, nbytes=4 * width * hidden,
    )
    outputs_recv = swap(outputs_part, "hid", 1)
    (full,) = call(
        outputs_body, [((owned, width), bf16)],
        outputs_part, outputs_recv, name="slot_outputs", nbytes=8 * owned * width,
    )

    far = [(over, 0) for over in range(2, rows)]
    near = [(1, 0)] + [(0, across) for across in range(1, blocks)]
    flights = []

    def fly(value, moves, came=None):
        came = came or moves
        flights.append((swap_by_core(value, moves), came))
        return flights[-1][0]

    passed = []
    for at in range(0, len(far), 2):
        moves = far[at : at + 2]
        got = fly(full, moves)
        passed += [(got, moves)]
    for at in range(0, len(near), 2):
        fly(full, near[at : at + 2])
    for across in range(1, blocks):
        fly(full, [(1, across)] * 2)
    direct = len(flights)
    held = lax.optimization_barrier([got for got, _ in passed] + [got for got, came in flights if came[0] == came[1]])
    passed = [(got, moves) for got, (_, moves) in zip(held, passed)]
    for got, moves in passed:
        for across in range(1, blocks):
            fly(got, [(0, across)] * 2, [(over, across) for over, _ in moves])
    def both(flights):
        pieces = []
        for got, came in flights:
            pieces += [got] if came[0] == came[1] else [got, swap(got, "hid", 1)]
        return pieces, [came for _, came in flights]

    pieces, plan = both(flights[:direct])
    numer, denom = call(
        functools.partial(combine_first_body, blocks, slots, plan),
        [((count, width), f32), ((count, 128), f32)],
        *lows, full, *pieces,
        name="combine_first", flops=2 * count * width * slots * blocks, nbytes=8 * count * width,
        scratch=[pltpu.VMEM((blocks * slots, width), bf16)],
    )
    pieces, plan = both(flights[direct:])
    tile = count // 2
    return pl.pallas_call(
        functools.partial(combine_last_body, blocks, slots, owned, plan),
        out_shape=jax.ShapeDtypeStruct((count, width), f32),
        grid=(count // tile,),
        in_specs=[pl.BlockSpec((tile, part), lambda i: (i, 0))] * (2 * blocks - 2)
        + [pl.BlockSpec((tile, width), lambda i: (i, 0)), pl.BlockSpec((tile, 128), lambda i: (i, 0))]
        + [VMEM] * len(pieces),
        out_specs=pl.BlockSpec((tile, width), lambda i: (i, 0)),
        scratch_shapes=[pltpu.VMEM(((blocks - 1) * slots, width), bf16)],
        name="combine_last",
        compiler_params=pltpu.CompilerParams(vmem_limit_bytes=24 * 2**20),
    )(*lows[2:], numer, denom, *pieces)


def solution(mesh):
    in_specs = (
        P(("groups", "tok", "slot", "hid"), None),
        P("groups", "slot"),
        P(("groups", "slot"), "tok", None, "hid"),
        P(("groups", "slot"), "tok", "hid", None),
    )
    out_specs = P(("groups", "tok", "slot", "hid"), None)
    return jax.shard_map(local, mesh=mesh, in_specs=in_specs, out_specs=out_specs, check_vma=False)
```

```python
import functools

import jax
import jax.numpy as jnp
from jax import lax
from jax.experimental import pallas as pl
from jax.experimental.pallas import tpu as pltpu
from jax.sharding import PartitionSpec as P

epsilon = 1e-06
bf16, f32 = jnp.bfloat16, jnp.float32
VMEM = pl.BlockSpec(memory_space=pltpu.VMEM)
STAY = pl.BlockSpec(memory_space=pltpu.HBM)
AXES = ("tok", "slot", "hid")


def call(body, outs, *args, name, flops=0, nbytes=0, stay=0, scratch=()):
    return pl.pallas_call(
        body,
        out_shape=[jax.ShapeDtypeStruct(s, d) for s, d in outs],
        in_specs=[VMEM] * (len(args) - stay) + [STAY] * stay,
        out_specs=[VMEM] * len(outs),
        scratch_shapes=list(scratch),
        name=name,
        compiler_params=pltpu.CompilerParams(vmem_limit_bytes=24 * 2**20),
        cost_estimate=pl.CostEstimate(flops=flops, bytes_accessed=nbytes, transcendentals=0),
    )(*args)


def swap(value, axis, step):
    return lax.ppermute(value, axis, [(i, i ^ step) for i in range(lax.axis_size(axis))])


def swap_by_core(value, moves):
    rows, blocks = lax.axis_size("tok"), lax.axis_size("slot")
    pairs = []
    for row in range(rows):
        for block in range(blocks):
            for core, (over, across) in enumerate(moves):
                to = (row ^ over) * blocks + (block ^ across)
                pairs.append(((row * blocks + block) * 2 + core, to * 2 + core))
    return lax.ppermute(value, AXES, pairs)


def spread(value, step, across):
    rows, blocks = lax.axis_size("tok"), lax.axis_size("slot")
    per = rows // 2
    pairs = []
    for row in range(rows):
        for block in range(blocks):
            for core in range(2):
                to = (core * per + (row % per ^ step)) * blocks + (block ^ across)
                pairs.append(((row * blocks + block) * 2 + core, to * 2 + (row // per ^ core)))
    return lax.ppermute(value, AXES, pairs)


def keys_body(key_ref, out_ref, sem):
    part = out_ref.shape[1]
    core = lax.axis_index("hid")
    copy = pltpu.make_async_copy(key_ref.at[:, pl.ds(pl.multiple_of(core * part, part), part)], out_ref, sem)
    copy.start()
    copy.wait()


def stage_body(after_ref, from_ref, here_ref, sem):
    copy = pltpu.make_async_copy(from_ref, here_ref, sem)
    copy.start()
    copy.wait()


def stage(after, value):
    return call(stage_body, [(value.shape, value.dtype)], after, value, name="stage", nbytes=4 * value.size, stay=1, scratch=[pltpu.SemaphoreType.DMA])[0]


def dispatch_body(first, owned, *refs):
    if first:
        tok_refs, key_ref, low_refs, scale_refs, piece_refs, numer_ref = refs[0:2], refs[2], refs[3:5], refs[5:7], refs[8:-1], refs[-1]
        refs[7][...] = tok_refs[0][...]
    else:
        tok_refs, key_ref, scale_refs, low_refs, piece_refs, numer_ref = refs[0:2], refs[2], refs[3:5], refs[5:7], refs[7:-1], refs[-1]
    width, part = key_ref.shape
    key = key_ref[...].astype(f32)
    key_scale = lax.rsqrt(jnp.sum(key * key, axis=0, keepdims=True) / width + epsilon)
    numer = None
    total = None
    for tok_ref, low_ref, scale_ref in zip(tok_refs, low_refs, scale_refs):
        if first:
            tok = tok_ref[...].astype(f32)
            scale = lax.rsqrt(jnp.sum(tok * tok, axis=1, keepdims=True) / width + epsilon) * (4.0 / width)
            scale_ref[...] = jnp.broadcast_to(scale, scale_ref.shape)
        else:
            scale = scale_ref[:, 0:1]
        logits = jnp.dot(tok_ref[...], key_ref[...], preferred_element_type=f32)
        weights = jnp.exp(logits * scale * key_scale)
        low = weights.astype(bf16)
        low_ref[...] = low
        mine = lax.dot_general(low, tok_ref[...], (((0,), (0,)), ((), ())), preferred_element_type=f32)
        numer = mine if numer is None else numer + mine
        mine = jnp.sum(weights, axis=0, keepdims=True)
        total = mine if total is None else total + mine
    numer_ref[...] = numer
    terms = []
    for _ in range(3):
        term = total.astype(bf16)
        terms.append(term)
        total = total - term.astype(f32)
    per = part // owned
    low_row = lax.rem(lax.axis_index("tok"), per)
    for step, ref in enumerate(piece_refs):
        start = pl.multiple_of((low_row ^ step) * owned, owned)
        ref[0:owned, :] = numer_ref[pl.ds(start, owned), :].astype(bf16)
        ref[owned:, :] = jnp.zeros((8, width), bf16)
        for index, term in enumerate(terms):
            ref[owned + index : owned + index + 1, 0:part] = term


def sum_body(*refs):
    piece_refs, out_ref = refs[:-1], refs[-1]
    out = None
    for ref in piece_refs:
        piece = ref[...].astype(f32)
        out = piece if out is None else out + piece
    out_ref[...] = out


def expert_body(part, mine_ref, other_ref, in_ref, out_w_ref, out_ref):
    owned = out_ref.shape[0]
    numer = mine_ref[0:owned, :] + other_ref[0:owned, :]
    total = mine_ref[owned:, 0:part] + other_ref[owned:, 0:part]
    total = total[0:1, :] + total[1:2, :] + total[2:3, :]
    per = part // owned
    lane = lax.broadcasted_iota(jnp.int32, (owned, part), 1)
    wanted = lax.broadcasted_iota(jnp.int32, (owned, part), 0) + lax.rem(lax.axis_index("tok"), per) * owned
    denom = jnp.sum(jnp.where(lane == wanted, jnp.broadcast_to(total, (owned, part)), 0.0), axis=1, keepdims=True)
    inputs = (numer / denom).astype(bf16)
    value = jnp.dot(inputs, in_ref[...], preferred_element_type=f32)
    hidden = jax.nn.gelu(value, approximate=True).astype(bf16)
    out_ref[...] = jnp.dot(hidden, out_w_ref[...], preferred_element_type=f32)


def outputs_body(part_ref, recv_ref, full_ref):
    full_ref[...] = (part_ref[...] + recv_ref[...]).astype(bf16)


def gather_pieces(all_ref, pieces, plan, slots, owned, first):
    core = lax.axis_index("hid")
    row = lax.axis_index("tok")
    pieces = list(pieces)

    def put(ref, starts, turn):
        start = jnp.where(core == turn, starts[0], starts[1])
        all_ref[pl.ds(pl.multiple_of(start, owned), owned), :] = ref[...]

    for moves in plan:
        starts = [(across - first) * slots + (row ^ over) * owned for over, across in moves]
        put(pieces.pop(0), starts, 0)
        if moves[0] != moves[1]:
            put(pieces.pop(0), starts, 1)


def mix(low_refs, all_ref, blocks, slots):
    part = slots // 2
    core = lax.axis_index("hid")
    numer = None
    for index, ref in enumerate(low_refs):
        start = (index // 2) * slots + (core if index % 2 == 0 else 1 - core) * part
        mine = jnp.dot(ref[...], all_ref[pl.ds(pl.multiple_of(start, part), part), :], preferred_element_type=f32)
        numer = mine if numer is None else numer + mine
    return numer


def combine_first_body(blocks, slots, plan, *refs):
    low_refs, full_ref, pieces = refs[: 2 * blocks], refs[2 * blocks], refs[2 * blocks + 1 : -3]
    numer_ref, denom_ref, all_ref = refs[-3:]
    all_ref[...] = jnp.zeros_like(all_ref)
    gather_pieces(all_ref, (full_ref,) + pieces, [((0, 0), (0, 0))] + plan, slots, full_ref.shape[0], 0)
    numer_ref[...] = mix(low_refs, all_ref, blocks, slots)
    denom = None
    for ref in low_refs:
        total = jnp.sum(ref[...].astype(f32), axis=1, keepdims=True)
        denom = total if denom is None else denom + total
    denom_ref[...] = jnp.broadcast_to(denom, denom_ref.shape)


def combine_last_body(blocks, slots, owned, tiles, plan, *refs):
    lows = 2 * (blocks - 1)
    low_refs, numer_ref, denom_ref, pieces = refs[:lows], refs[lows], refs[lows + 1], refs[lows + 2 : -4]
    out_hbm, all_ref, out_ref, sems = refs[-4:]
    part = slots // 2
    per = part // owned
    core = lax.axis_index("hid")
    far = 1 - lax.axis_index("tok") // per
    if per > 2:
        all_ref[...] = jnp.zeros_like(all_ref)
    gather_pieces(all_ref, pieces, plan, slots, owned, 1)
    tile = out_ref.shape[0] // tiles
    copies = []
    for index in range(tiles):
        rows = pl.ds(index * tile, tile)
        numer = numer_ref[rows, :]
        for block in range(blocks - 1):
            mine, other = low_refs[2 * block][rows, :], low_refs[2 * block + 1][rows, :]
            for side in [far] if per == 2 else [0, 1]:
                low = jnp.where(core == side, mine, other)
                start = pl.multiple_of(block * slots + side * part, part)
                numer = numer + jnp.dot(low, all_ref[pl.ds(start, part), :], preferred_element_type=f32)
        out_ref[rows, :] = numer / denom_ref[rows, 0:1]
        copies.append(pltpu.make_async_copy(out_ref.at[rows, :], out_hbm.at[rows, :], sems.at[index]))
        copies[-1].start()
    for copy in copies:
        copy.wait()


def local(tokens, slot_keys, w_in, w_out):
    count, width = tokens.shape
    slots = slot_keys.shape[1]
    hidden = w_in.shape[3]
    rows, blocks = lax.axis_size("tok"), lax.axis_size("slot")
    owned = slots // rows
    part = slots // 2
    mac = 8 * count * width * part
    piece = ((owned + 8, width), bf16)
    lows_shape = [((count, part), bf16)] * 2
    scratch = [pltpu.VMEM((part, width), f32)]

    (keys,) = call(keys_body, [((width, part), bf16)], slot_keys, name="keys", nbytes=4 * width * part, stay=1, scratch=[pltpu.SemaphoreType.DMA])
    arrived = [swap(keys, "slot", across) for across in range(1, blocks)]
    beside = swap(tokens, "hid", 1)
    low_mine, low_send, scale, scale_beside, here, *pieces = call(
        functools.partial(dispatch_body, True, owned),
        lows_shape + [((count, 128), f32)] * 2 + [((count, width), bf16)] + [piece] * (rows // 2),
        tokens, beside, keys, name="dispatch_own", flops=mac, nbytes=4 * count * width, scratch=scratch,
    )
    sent = [spread(value, step, 0) for step, value in enumerate(pieces)]
    lows = [low_mine, swap(low_send, "hid", 1)]
    for across in range(1, blocks):
        low_mine, low_send, *pieces = call(
            functools.partial(dispatch_body, False, owned),
            lows_shape + [piece] * (rows // 2),
            here, beside, arrived[across - 1], scale, scale_beside,
            name="dispatch_other", flops=mac, nbytes=4 * count * width, scratch=scratch,
        )
        sent += [spread(value, step, across) for step, value in enumerate(pieces)]
        lows += [low_mine, swap(low_send, "hid", 1)]
    out_here = stage(low_send, w_out[0, 0])
    sent, lows, out_here = lax.optimization_barrier((sent, lows, out_here))
    (mine,) = call(sum_body, [((owned + 8, width), f32)], *sent, name="sum_pieces", nbytes=4 * owned * width * len(sent))
    other = swap(mine, "hid", 1)
    (outputs_part,) = call(
        functools.partial(expert_body, part), [((owned, width), f32)],
        mine, other, w_in[0, 0], out_here,
        name="expert", flops=4 * owned * width * hidden, nbytes=4 * width * hidden,
    )
    outputs_recv = swap(outputs_part, "hid", 1)
    (full,) = call(
        outputs_body, [((owned, width), bf16)],
        outputs_part, outputs_recv, name="slot_outputs", nbytes=8 * owned * width,
    )

    far = [(over, 0) for over in range(2, rows)]
    near = [(1, 0)] + [(0, across) for across in range(1, blocks)]
    flights = []

    def fly(value, moves, came=None):
        came = came or moves
        flights.append((swap_by_core(value, moves), came))
        return flights[-1][0]

    passed = []
    for at in range(0, len(far), 2):
        moves = far[at : at + 2]
        got = fly(full, moves)
        passed += [(got, moves)]
    for at in range(0, len(near), 2):
        fly(full, near[at : at + 2])
    for across in range(1, blocks):
        fly(full, [(1, across)] * 2)
    direct = len(flights)
    held = lax.optimization_barrier([got for got, _ in passed] + [got for got, came in flights if came[0] == came[1]])
    passed = [(got, moves) for got, (_, moves) in zip(held, passed)]
    for got, moves in passed:
        for across in range(1, blocks):
            fly(got, [(0, across)] * 2, [(over, across) for over, _ in moves])
    def both(flights):
        pieces = []
        for got, came in flights:
            pieces += [got] if came[0] == came[1] else [got, swap(got, "hid", 1)]
        return pieces, [came for _, came in flights]

    pieces, plan = both(flights[:direct])
    numer, denom = call(
        functools.partial(combine_first_body, blocks, slots, plan),
        [((count, width), f32), ((count, 128), f32)],
        *lows, full, *pieces,
        name="combine_first", flops=2 * count * width * slots * blocks, nbytes=8 * count * width,
        scratch=[pltpu.VMEM((blocks * slots, width), bf16)],
    )
    pieces, plan = both(flights[direct:])
    tiles = 4
    return pl.pallas_call(
        functools.partial(combine_last_body, blocks, slots, owned, tiles, plan),
        out_shape=jax.ShapeDtypeStruct((count, width), f32),
        in_specs=[VMEM] * (2 * blocks + len(pieces)),
        out_specs=pl.BlockSpec(memory_space=pl.ANY),
        scratch_shapes=[
            pltpu.VMEM(((blocks - 1) * slots, width), bf16),
            pltpu.VMEM((count, width), f32),
            pltpu.SemaphoreType.DMA((tiles,)),
        ],
        name="combine_last",
        compiler_params=pltpu.CompilerParams(vmem_limit_bytes=24 * 2**20),
    )(*lows[2:], numer, denom, *pieces)


def solution(mesh):
    in_specs = (
        P(("groups", "tok", "slot", "hid"), None),
        P("groups", "slot"),
        P(("groups", "slot"), "tok", None, "hid"),
        P(("groups", "slot"), "tok", "hid", None),
    )
    out_specs = P(("groups", "tok", "slot", "hid"), None)
    return jax.shard_map(local, mesh=mesh, in_specs=in_specs, out_specs=out_specs, check_vma=False)
```

```python
import functools

import jax
import jax.numpy as jnp
from jax import lax
from jax.experimental import pallas as pl
from jax.experimental.pallas import tpu as pltpu
from jax.sharding import PartitionSpec as P

epsilon = 1e-06
bf16, f32 = jnp.bfloat16, jnp.float32
VMEM = pl.BlockSpec(memory_space=pltpu.VMEM)
STAY = pl.BlockSpec(memory_space=pltpu.HBM)
AXES = ("tok", "slot", "hid")


def call(body, outs, *args, name, flops=0, nbytes=0, stay=0, scratch=()):
    return pl.pallas_call(
        body,
        out_shape=[jax.ShapeDtypeStruct(s, d) for s, d in outs],
        in_specs=[VMEM] * (len(args) - stay) + [STAY] * stay,
        out_specs=[VMEM] * len(outs),
        scratch_shapes=list(scratch),
        name=name,
        compiler_params=pltpu.CompilerParams(vmem_limit_bytes=24 * 2**20),
        cost_estimate=pl.CostEstimate(flops=flops, bytes_accessed=nbytes, transcendentals=0),
    )(*args)


def swap(value, axis, step):
    return lax.ppermute(value, axis, [(i, i ^ step) for i in range(lax.axis_size(axis))])


def swap_by_core(value, moves):
    rows, blocks = lax.axis_size("tok"), lax.axis_size("slot")
    pairs = []
    for row in range(rows):
        for block in range(blocks):
            for core, (over, across) in enumerate(moves):
                to = (row ^ over) * blocks + (block ^ across)
                pairs.append(((row * blocks + block) * 2 + core, to * 2 + core))
    return lax.ppermute(value, AXES, pairs)


def spread(value, step, across):
    rows, blocks = lax.axis_size("tok"), lax.axis_size("slot")
    per = rows // 2
    pairs = []
    for row in range(rows):
        for block in range(blocks):
            for core in range(2):
                to = (core * per + (row % per ^ step)) * blocks + (block ^ across)
                pairs.append(((row * blocks + block) * 2 + core, to * 2 + (row // per ^ core)))
    return lax.ppermute(value, AXES, pairs)


def keys_body(key_ref, out_ref, sem):
    part = out_ref.shape[1]
    core = lax.axis_index("hid")
    copy = pltpu.make_async_copy(key_ref.at[:, pl.ds(pl.multiple_of(core * part, part), part)], out_ref, sem)
    copy.start()
    copy.wait()


def stage_body(after_ref, from_ref, here_ref, sem):
    copy = pltpu.make_async_copy(from_ref, here_ref, sem)
    copy.start()
    copy.wait()


def stage(after, value):
    return call(stage_body, [(value.shape, value.dtype)], after, value, name="stage", nbytes=4 * value.size, stay=1, scratch=[pltpu.SemaphoreType.DMA])[0]


def dispatch_body(first, owned, *refs):
    if first:
        tok_refs, key_ref, low_refs, scale_refs, piece_refs, numer_ref = refs[0:2], refs[2], refs[3:5], refs[5:7], refs[8:-1], refs[-1]
        refs[7][...] = tok_refs[0][...]
    else:
        tok_refs, key_ref, scale_refs, low_refs, piece_refs, numer_ref = refs[0:2], refs[2], refs[3:5], refs[5:7], refs[7:-1], refs[-1]
    width, part = key_ref.shape
    key = key_ref[...].astype(f32)
    key_scale = lax.rsqrt(jnp.sum(key * key, axis=0, keepdims=True) / width + epsilon)
    numer = None
    total = None
    for tok_ref, low_ref, scale_ref in zip(tok_refs, low_refs, scale_refs):
        if first:
            tok = tok_ref[...].astype(f32)
            scale = lax.rsqrt(jnp.sum(tok * tok, axis=1, keepdims=True) / width + epsilon) * (4.0 / width)
            scale_ref[...] = jnp.broadcast_to(scale, scale_ref.shape)
        else:
            scale = scale_ref[:, 0:1]
        logits = jnp.dot(tok_ref[...], key_ref[...], preferred_element_type=f32)
        weights = jnp.exp(logits * scale * key_scale)
        low = weights.astype(bf16)
        low_ref[...] = low
        mine = lax.dot_general(low, tok_ref[...], (((0,), (0,)), ((), ())), preferred_element_type=f32)
        numer = mine if numer is None else numer + mine
        mine = jnp.sum(weights, axis=0, keepdims=True)
        total = mine if total is None else total + mine
    numer_ref[...] = numer
    terms = []
    for _ in range(3):
        term = total.astype(bf16)
        terms.append(term)
        total = total - term.astype(f32)
    per = part // owned
    low_row = lax.rem(lax.axis_index("tok"), per)
    for step, ref in enumerate(piece_refs):
        start = pl.multiple_of((low_row ^ step) * owned, owned)
        ref[0:owned, :] = numer_ref[pl.ds(start, owned), :].astype(bf16)
        ref[owned:, :] = jnp.zeros((8, width), bf16)
        for index, term in enumerate(terms):
            ref[owned + index : owned + index + 1, 0:part] = term


def sum_body(*refs):
    piece_refs, out_ref = refs[:-1], refs[-1]
    out = None
    for ref in piece_refs:
        piece = ref[...].astype(f32)
        out = piece if out is None else out + piece
    out_ref[...] = out


def expert_body(part, mine_ref, other_ref, in_ref, out_w_ref, out_ref):
    owned = out_ref.shape[0]
    numer = mine_ref[0:owned, :] + other_ref[0:owned, :]
    total = mine_ref[owned:, 0:part] + other_ref[owned:, 0:part]
    total = total[0:1, :] + total[1:2, :] + total[2:3, :]
    per = part // owned
    lane = lax.broadcasted_iota(jnp.int32, (owned, part), 1)
    wanted = lax.broadcasted_iota(jnp.int32, (owned, part), 0) + lax.rem(lax.axis_index("tok"), per) * owned
    denom = jnp.sum(jnp.where(lane == wanted, jnp.broadcast_to(total, (owned, part)), 0.0), axis=1, keepdims=True)
    inputs = (numer / denom).astype(bf16)
    value = jnp.dot(inputs, in_ref[...], preferred_element_type=f32)
    hidden = jax.nn.gelu(value, approximate=True).astype(bf16)
    out_ref[...] = jnp.dot(hidden, out_w_ref[...], preferred_element_type=f32)


def outputs_body(part_ref, recv_ref, full_ref):
    full_ref[...] = (part_ref[...] + recv_ref[...]).astype(bf16)


def gather_pieces(all_ref, pieces, plan, slots, owned, first):
    core = lax.axis_index("hid")
    row = lax.axis_index("tok")
    pieces = list(pieces)

    def put(ref, starts, turn):
        start = jnp.where(core == turn, starts[0], starts[1])
        all_ref[pl.ds(pl.multiple_of(start, owned), owned), :] = ref[...]

    for moves in plan:
        starts = [(across - first) * slots + (row ^ over) * owned for over, across in moves]
        put(pieces.pop(0), starts, 0)
        if moves[0] != moves[1]:
            put(pieces.pop(0), starts, 1)


def mix(low_refs, all_ref, blocks, slots):
    part = slots // 2
    core = lax.axis_index("hid")
    numer = None
    for index, ref in enumerate(low_refs):
        start = (index // 2) * slots + (core if index % 2 == 0 else 1 - core) * part
        mine = jnp.dot(ref[...], all_ref[pl.ds(pl.multiple_of(start, part), part), :], preferred_element_type=f32)
        numer = mine if numer is None else numer + mine
    return numer


def combine_first_body(blocks, slots, plan, *refs):
    low_refs, full_ref, pieces = refs[: 2 * blocks], refs[2 * blocks], refs[2 * blocks + 1 : -3]
    numer_ref, denom_ref, all_ref = refs[-3:]
    all_ref[...] = jnp.zeros_like(all_ref)
    gather_pieces(all_ref, (full_ref,) + pieces, [((0, 0), (0, 0))] + plan, slots, full_ref.shape[0], 0)
    numer_ref[...] = mix(low_refs, all_ref, blocks, slots)
    denom = None
    for ref in low_refs:
        total = jnp.sum(ref[...].astype(f32), axis=1, keepdims=True)
        denom = total if denom is None else denom + total
    denom_ref[...] = jnp.broadcast_to(denom, denom_ref.shape)


def combine_last_body(blocks, slots, owned, tiles, plan, *refs):
    lows = 2 * (blocks - 1)
    low_refs, numer_ref, denom_ref, pieces = refs[:lows], refs[lows], refs[lows + 1], refs[lows + 2 : -4]
    out_hbm, all_ref, out_ref, sems = refs[-4:]
    part = slots // 2
    per = part // owned
    core = lax.axis_index("hid")
    far = 1 - lax.axis_index("tok") // per
    if per > 2:
        all_ref[...] = jnp.zeros_like(all_ref)
    gather_pieces(all_ref, pieces, plan, slots, owned, 1)
    tile = out_ref.shape[0] // tiles
    copies = []
    for index in range(tiles):
        rows = pl.ds(index * tile, tile)
        numer = numer_ref[rows, :]
        for block in range(blocks - 1):
            mine, other = low_refs[2 * block][rows, :], low_refs[2 * block + 1][rows, :]
            for side in [far] if per == 2 else [0, 1]:
                low = jnp.where(core == side, mine, other)
                start = pl.multiple_of(block * slots + side * part, part)
                numer = numer + jnp.dot(low, all_ref[pl.ds(start, part), :], preferred_element_type=f32)
        out_ref[rows, :] = numer / denom_ref[rows, 0:1]
        copies.append(pltpu.make_async_copy(out_ref.at[rows, :], out_hbm.at[rows, :], sems.at[index]))
        copies[-1].start()
    for copy in copies:
        copy.wait()


def local(tokens, slot_keys, w_in, w_out):
    count, width = tokens.shape
    slots = slot_keys.shape[1]
    hidden = w_in.shape[3]
    rows, blocks = lax.axis_size("tok"), lax.axis_size("slot")
    owned = slots // rows
    part = slots // 2
    mac = 8 * count * width * part
    piece = ((owned + 8, width), bf16)
    lows_shape = [((count, part), bf16)] * 2
    scratch = [pltpu.VMEM((part, width), f32)]

    (keys,) = call(keys_body, [((width, part), bf16)], slot_keys, name="keys", nbytes=4 * width * part, stay=1, scratch=[pltpu.SemaphoreType.DMA])
    arrived = [swap(keys, "slot", across) for across in range(1, blocks)]
    beside = swap(tokens, "hid", 1)
    low_mine, low_send, scale, scale_beside, here, *pieces = call(
        functools.partial(dispatch_body, True, owned),
        lows_shape + [((count, 128), f32)] * 2 + [((count, width), bf16)] + [piece] * (rows // 2),
        tokens, beside, keys, name="dispatch_own", flops=mac, nbytes=4 * count * width, scratch=scratch,
    )
    sent = [spread(value, step, 0) for step, value in list(enumerate(pieces))[::-1]]
    lows = [low_mine, swap(low_send, "hid", 1)]
    for across in range(1, blocks):
        low_mine, low_send, *pieces = call(
            functools.partial(dispatch_body, False, owned),
            lows_shape + [piece] * (rows // 2),
            here, beside, arrived[across - 1], scale, scale_beside,
            name="dispatch_other", flops=mac, nbytes=4 * count * width, scratch=scratch,
        )
        sent += [spread(value, step, across) for step, value in enumerate(pieces)]
        lows += [low_mine, swap(low_send, "hid", 1)]
    out_here = stage(low_send, w_out[0, 0])
    sent, lows, out_here = lax.optimization_barrier((sent, lows, out_here))
    (mine,) = call(sum_body, [((owned + 8, width), f32)], *sent, name="sum_pieces", nbytes=4 * owned * width * len(sent))
    other = swap(mine, "hid", 1)
    (outputs_part,) = call(
        functools.partial(expert_body, part), [((owned, width), f32)],
        mine, other, w_in[0, 0], out_here,
        name="expert", flops=4 * owned * width * hidden, nbytes=4 * width * hidden,
    )
    outputs_recv = swap(outputs_part, "hid", 1)
    (full,) = call(
        outputs_body, [((owned, width), bf16)],
        outputs_part, outputs_recv, name="slot_outputs", nbytes=8 * owned * width,
    )

    far = [(over, 0) for over in range(2, rows)]
    near = [(0, 1), (1, 1)] if blocks == 2 else [(1, 0)] + [(0, across) for across in range(1, blocks)]
    flights = []

    def fly(value, moves, came=None):
        came = came or moves
        flights.append((swap_by_core(value, moves), came))
        return flights[-1][0]

    passed = []
    for at in range(0, len(far), 2):
        moves = far[at : at + 2]
        got = fly(full, moves)
        passed += [(got, moves)]
    for at in range(0, len(near), 2):
        fly(full, near[at : at + 2])
    for across in range(1, blocks):
        fly(full, [(1, 0)] * 2) if blocks == 2 else fly(full, [(1, across)] * 2)
    direct = len(flights)
    held = lax.optimization_barrier([got for got, _ in passed] + [got for got, came in flights if came[0] == came[1]])
    passed = [(got, moves) for got, (_, moves) in zip(held, passed)]
    for got, moves in passed:
        for across in range(1, blocks):
            fly(got, [(0, across)] * 2, [(over, across) for over, _ in moves])
    def both(flights):
        pieces = []
        for got, came in flights:
            pieces += [got] if came[0] == came[1] else [got, swap(got, "hid", 1)]
        return pieces, [came for _, came in flights]

    pieces, plan = both(flights[:direct])
    numer, denom = call(
        functools.partial(combine_first_body, blocks, slots, plan),
        [((count, width), f32), ((count, 128), f32)],
        *lows, full, *pieces,
        name="combine_first", flops=2 * count * width * slots * blocks, nbytes=8 * count * width,
        scratch=[pltpu.VMEM((blocks * slots, width), bf16)],
    )
    pieces, plan = both(flights[direct:])
    tiles = 4
    return pl.pallas_call(
        functools.partial(combine_last_body, blocks, slots, owned, tiles, plan),
        out_shape=jax.ShapeDtypeStruct((count, width), f32),
        in_specs=[VMEM] * (2 * blocks + len(pieces)),
        out_specs=pl.BlockSpec(memory_space=pl.ANY),
        scratch_shapes=[
            pltpu.VMEM(((blocks - 1) * slots, width), bf16),
            pltpu.VMEM((count, width), f32),
            pltpu.SemaphoreType.DMA((tiles,)),
        ],
        name="combine_last",
        compiler_params=pltpu.CompilerParams(vmem_limit_bytes=24 * 2**20),
    )(*lows[2:], numer, denom, *pieces)


def solution(mesh):
    in_specs = (
        P(("groups", "tok", "slot", "hid"), None),
        P("groups", "slot"),
        P(("groups", "slot"), "tok", None, "hid"),
        P(("groups", "slot"), "tok", "hid", None),
    )
    out_specs = P(("groups", "tok", "slot", "hid"), None)
    return jax.shard_map(local, mesh=mesh, in_specs=in_specs, out_specs=out_specs, check_vma=False)
```
